32 devices in a mesh: groups: 2 (over x), ctx: 8 (over z, y), exp: 2 (over core).
Axes of the slice: x: 2, y: 2, z: 4, core: 2. Of those that a mesh axis runs over, the one named last changes fastest.
Arguments:
- tokens: bfloat16 [2048, 5120], P(('groups', 'ctx'), 'exp'), parts along dimension 0, may hold values from -6 to 6
- route_ids: int32 [2048, 2], P(('groups', 'ctx')), parts along dimension 0, may hold values from 0 to 3, all different within a row; in each aligned block of 128 rows (0 to 127, 128 to 255, ...) at most 128 rows name the same one
- route_gates: float32 [2048, 2], P(('groups', 'ctx')), parts along dimension 0, may hold values from 0.2 to 1
- w_in: bfloat16 [8, 5120, 1536], P('ctx', 'exp'), may hold values from -0.078125 to 0.078125
- w_out: bfloat16 [8, 768, 5120], P('ctx', None, 'exp'), may hold values from -0.15625 to 0.15625
Outputs:
- mixed: bfloat16 [2048, 5120], P(('groups', 'ctx'), 'exp'), parts along dimension 0
The draws below stay inside these ranges and needn't reach their ends.
There are 2 independent parts, one for each index of `groups`. The reference program is written for one: setup_inputs(seed, part) draws one part's arguments, and reference() takes and returns one part's arrays. A program takes and returns all parts, laid end to end along the dimension named above; an argument that names none is the same for every part. Nothing has to cross between parts.
Inputs may be any that keep to these rules, and one draw needn't show every extreme that they name: `route_ids`: within the 128 rows of one device no expert is named more than 128 times, a bound that some block reaches; the ids of one token differ.
All inputs are finite; a program needn't handle non-finite values.
Results may differ from the reference program's by a relative error of at most 0.025.
Values may be sent and summed in bfloat16 or wider, within the bound.
A program may use at most 64 MiB of HBM per device.

```python
import math
import jax
import jax.numpy as jnp
import numpy as np
from jax import lax

D = 5120
FF = 1536
TOK_DEV = 128
TOPW = 2
FH = 768
EXPERTS = 4
CAP = 128
TOKENS = 1024
N_CTX = 8


def levels(rng, dims, split, low, top_value):
    level = 1.0
    for axis_at, shards_of in split:
        steps = jax.random.uniform(jax.random.fold_in(jax.random.fold_in(rng, 6), axis_at), (shards_of,), jnp.float32, low / len(split), top_value / len(split))
        level = level * jnp.repeat(jnp.exp(steps), dims[axis_at] // shards_of).reshape((-1,) + (1,) * (len(dims) - 1 - axis_at))
    return level


def routed_block(own_key, own, number, rows, count, top, most, slope):
    order = jax.random.permutation(own_key, count)
    packed, common = shares(count, rows * top, most, slope, True), shares(count, rows * top, most, slope, False)
    places = jnp.arange(count)

    def named(tallies, offset_by):
        used = int((tallies > 0).sum())
        fixed = max(1, used // 4)
        shifted = fixed + (places - fixed + offset_by * (used - fixed)) % max(1, count - fixed)
        return jnp.zeros((count,), jnp.int32).at[order[jnp.where(places < fixed, places, shifted)]].set(jnp.asarray(tallies, jnp.int32))

    tallies = jnp.where(number % 4 == 0, named(packed, number // 4), named(common, number - number // 4 - 1))
    mixed = jax.random.permutation(jax.random.fold_in(own, 3), count)
    donor, receiver = mixed[0:count // 2 * 2:2], mixed[1:count // 2 * 2:2]
    slack = jnp.minimum(tallies[donor] - 1, most - tallies[receiver]) // 2
    slack = jnp.where((donor == order[0]) | (receiver == order[0]) | (tallies[receiver] == 0), 0, jnp.maximum(slack, 0))
    shifted = jax.random.randint(jax.random.fold_in(own, 4), (count // 2,), 0, 1 << 20) % (slack + 1)
    tallies = tallies.at[donor].add(-shifted).at[receiver].add(shifted)
    items = jnp.searchsorted(jnp.cumsum(tallies), jnp.arange(rows * top), side="right").astype(jnp.int32)
    grid = items.reshape(top, rows).T
    grid = grid[jax.random.permutation(jax.random.fold_in(own, 1), rows)]
    offset_by = jax.random.randint(jax.random.fold_in(own, 2), (rows, 1), 0, top)
    return jnp.take_along_axis(grid, (jnp.arange(top)[None, :] + offset_by) % top, axis=1)


def shares(number_of, total, reach, skew, full):
    loads = [(1 << 20) // math.isqrt(rank ** skew) + 1 for rank in range(1, number_of + 1)]
    largest = reach if full else min(reach, max(-(-total // number_of), total * loads[0] // sum(loads)))
    least = 1 if total - largest >= number_of - 1 else 0
    counts, spare = [largest] + [least] * (number_of - 1), total - largest - least * (number_of - 1)
    while spare > 0:
        candidates = [i for i in range(1, number_of) if counts[i] < largest] or [i for i in range(1, number_of) if counts[i] < reach]
        pool, budget = sum([loads[i] for i in candidates]), spare
        for i in candidates:
            addition = min(reach - counts[i], max(1, budget * loads[i] // pool), spare)
            counts[i] = counts[i] + addition
            spare = spare - addition
    return np.array(counts)


def noise(rng, dims, spread, reach, pieces=(), kind=jnp.bfloat16):
    result = spread * jax.random.normal(rng, dims, jnp.float32)
    if pieces:
        result = result * levels(rng, dims, pieces, -0.22, 0.18)
    return jnp.clip(result, -reach, reach).astype(kind)


def setup_inputs(seed: int = 0, part: int = 0) -> dict:
    splits = jax.random.split(jax.random.key(seed), 6)
    part_splits = jax.random.split(jax.random.fold_in(splits[5], part), 6)
    tokens = noise(part_splits[0], (TOKENS, D), 1.0, 6.0, ((0, 8), (1, 2)))
    route_ids_keys = jax.random.split(jax.random.fold_in(part_splits[1], 1), TOKENS // TOK_DEV)
    route_ids_turns = jax.random.permutation(jax.random.fold_in(part_splits[1], 3), TOKENS // TOK_DEV)
    route_ids = jax.vmap(lambda own, number: routed_block(jax.random.fold_in(part_splits[1], 2), own, number, TOK_DEV, EXPERTS, TOPW, CAP, 2))(route_ids_keys, route_ids_turns).reshape((TOKENS, TOPW))
    route_gates = jnp.clip(jnp.exp(math.log(1.0) - 1.609438 * jax.random.uniform(part_splits[2], (TOKENS, TOPW), jnp.float32) ** levels(part_splits[2], (TOKENS, TOPW), ((0, 8),), -0.2, 0.2)), 0.2, 1.0)
    w_in = noise(splits[3], (2 * EXPERTS, D, 2 * FH), D ** -0.5, 0.078125, ((0, 8), (1, 2)))
    w_out = noise(splits[4], (2 * EXPERTS, FH, D), FF ** -0.5, 0.15625, ((0, 8), (2, 2)))
    return dict(tokens=tokens, route_ids=route_ids, route_gates=route_gates, w_in=w_in, w_out=w_out)


def round_keep(values):
    rounded = values.astype(jnp.bfloat16)
    rounded = lax.optimization_barrier(rounded)
    return rounded.astype(jnp.float32)


def reference(tokens, route_ids, route_gates, w_in, w_out):
    total, width = tokens.shape
    half = width // 2
    most = N_CTX * CAP
    flat_ids = route_ids.reshape(-1).astype(jnp.int32)
    flat_gates = route_gates.reshape(-1).astype(jnp.float32)
    top_count = route_ids.shape[1]

    def step(accum, expert):
        hits = flat_ids == expert
        picked = jnp.nonzero(hits, size=most, fill_value=0)[0].astype(jnp.int32)
        valid = jnp.arange(most, dtype=jnp.int32) < jnp.sum(hits.astype(jnp.int32))
        rows_index = (picked // top_count).astype(jnp.int32)
        rows = tokens[rows_index]
        output = jnp.zeros((most, width), jnp.float32)
        for part in range(2):
            weight_in = w_in[2 * expert + part]
            weight_out = w_out[2 * expert + part]
            lower = round_keep(jnp.dot(rows[:, :half], weight_in[:half], preferred_element_type=jnp.float32))
            upper = round_keep(jnp.dot(rows[:, half:], weight_in[half:], preferred_element_type=jnp.float32))
            summed = lower + upper
            hidden_units = weight_out.shape[0]
            hidden = (jax.nn.silu(summed[:, :hidden_units]) * summed[:, hidden_units:]).astype(jnp.bfloat16)
            output = output + round_keep(jnp.dot(hidden, weight_out, preferred_element_type=jnp.float32))
        value = round_keep(output)
        weight = jnp.where(valid, flat_gates[picked], jnp.float32(0.0))
        accum = accum.at[rows_index].add(weight[:, None] * value)
        return accum, None

    start = jnp.zeros((total, width), jnp.float32)
    accum = lax.scan(step, start, jnp.arange(EXPERTS, dtype=jnp.int32))[0]
    return accum.astype(jnp.bfloat16)
```

```python
import jax
import jax.numpy as jnp
from jax import lax
from jax.sharding import PartitionSpec as P


def expert_half(rows, w_in, w_out):
    gate_up = jnp.dot(rows, w_in[0], preferred_element_type=jnp.float32)
    summed = lax.psum(gate_up.astype(jnp.bfloat16), "exp").astype(jnp.float32)
    hidden_units = w_out.shape[1]
    hidden = (jax.nn.silu(summed[:, :hidden_units]) * summed[:, hidden_units:]).astype(jnp.bfloat16)
    return jnp.dot(hidden, w_out[0], preferred_element_type=jnp.float32).astype(jnp.bfloat16)


def gate_table(route_ids, route_gates, experts):
    named = route_ids[:, :, None] == jnp.arange(experts, dtype=jnp.int32)
    return jnp.sum(jnp.where(named, route_gates[:, :, None], 0.0), axis=1)


def dense(tokens, route_ids, route_gates, w_in, w_out):
    experts = lax.axis_size("ctx") // 2
    gates = lax.all_gather(gate_table(route_ids, route_gates, experts), "ctx", axis=0, tiled=True)
    gate = lax.dynamic_slice_in_dim(gates, lax.axis_index("ctx") // 2, 1, axis=1)
    rows = lax.all_gather(tokens, "ctx", axis=0, tiled=True)
    out = (expert_half(rows, w_in, w_out).astype(jnp.float32) * gate).astype(jnp.bfloat16)
    return lax.psum_scatter(out, "ctx", scatter_dimension=0, tiled=True)


def per_device(tokens, route_ids, route_gates, w_in, w_out):
    ctx_size = lax.axis_size("ctx")
    experts = ctx_size // 2
    tok_rows, half_width = tokens.shape
    top_count = route_ids.shape[1]
    capacity = 2 * ((top_count * tok_rows + experts - 1) // experts)
    if capacity >= tok_rows:
        return dense(tokens, route_ids, route_gates, w_in, w_out)
    slots = experts * capacity
    flat_ids = route_ids.reshape(-1)
    onehot = (flat_ids[:, None] == jnp.arange(experts, dtype=jnp.int32)[None, :]).astype(jnp.int32)
    before = jnp.cumsum(onehot, axis=0) - onehot
    rank = jnp.sum(before * onehot, axis=1)
    slot_of = flat_ids * capacity + rank
    placed = (slot_of[:, None] == jnp.arange(slots, dtype=jnp.int32)[None, :]).astype(jnp.bfloat16)
    placed = placed.reshape(tok_rows, top_count, slots)
    every_map = jnp.sum(placed.astype(jnp.float32), axis=1).astype(jnp.bfloat16)
    gathered = lax.dot_general(
        every_map, tokens, (((0,), (0,)), ((), ())), preferred_element_type=jnp.float32
    ).astype(jnp.bfloat16)
    outgoing = jnp.broadcast_to(
        gathered.reshape(experts, 1, capacity, half_width), (experts, 2, capacity, half_width)
    ).reshape(ctx_size, capacity, half_width)
    received = lax.all_to_all(outgoing, "ctx", split_axis=0, concat_axis=0, tiled=True)
    count = received.shape[1]
    partial_out = expert_half(received.reshape(-1, half_width), w_in, w_out).reshape(
        ctx_size, count, half_width
    )
    returned = lax.all_to_all(partial_out, "ctx", split_axis=0, concat_axis=0, tiled=True)
    results = (
        jnp.sum(returned.astype(jnp.float32).reshape(experts, 2, capacity, half_width), axis=1)
        .astype(jnp.bfloat16)
        .reshape(slots, half_width)
    )
    mixed = jnp.zeros((tok_rows, half_width), jnp.float32)
    for route in range(top_count):
        route_out = jnp.dot(placed[:, route], results, preferred_element_type=jnp.float32)
        mixed = mixed + route_gates[:, route : route + 1] * route_out
    return mixed.astype(jnp.bfloat16)


def solution(mesh):
    placed = (
        P(("groups", "ctx"), "exp"),
        P(("groups", "ctx"), None),
        P(("groups", "ctx"), None),
        P("ctx", "exp", None),
        P("ctx", None, "exp"),
    )
    return jax.shard_map(
        per_device,
        mesh=mesh,
        in_specs=placed,
        out_specs=P(("groups", "ctx"), "exp"),
        check_vma=False,
    )
```

```python
import functools

import jax
import jax.numpy as jnp
from jax import lax
from jax.experimental import pallas as pl
from jax.experimental.pallas import tpu as pltpu
from jax.sharding import PartitionSpec as P

MESH = pl.DeviceIdType.MESH


def ordered(z, planes, step):
    if step == 0:
        return z
    near = jnp.minimum(z, planes - 1 - z)
    paired = jnp.where(step % 2 == 1, z - (step + 1) // 2, z + (step + 1) // 2)
    rest = jnp.where(2 * z < planes - 1, z + step - near, z - step + near)
    return jnp.where(step <= 2 * near, paired, rest)


def layer_kernel(planes, tokens_hbm, gates_ref, w_in_hbm, w_out_hbm, mixed_ref,
                 w_in, w_out, rows, gates, mine, theirs, hidden, halves, from_y, to_z, from_z,
                 load_sem, gate_send, gate_recv, row_recv, up_send, down_send, y_send, mine_send, theirs_recv,
                 back_send, back_recv, out_send, out_recv, core_sem):
    ctx = 2 * planes
    me = lax.axis_index("ctx")
    core = lax.axis_index("exp")
    z, y = me // 2, me % 2
    side = z * 2 + 1 - y
    count, width = tokens_hbm.shape
    fh = w_out.shape[0]

    load_rows = pltpu.make_async_copy(tokens_hbm, rows.at[z, y], load_sem.at[0])
    load_in = pltpu.make_async_copy(w_in_hbm.at[0], w_in, load_sem.at[1])
    load_out = pltpu.make_async_copy(w_out_hbm.at[0], w_out, load_sem.at[2])
    load_gates = pltpu.make_async_copy(gates_ref, gates.at[me], load_sem.at[3])
    load_rows.start()
    load_gates.start()
    load_in.start()
    load_out.start()

    barrier = pltpu.get_barrier_semaphore()
    for step in range(1, ctx):
        pl.semaphore_signal(barrier, inc=1, device_id={"ctx": (me + step) % ctx}, device_id_type=MESH)
    pl.semaphore_signal(barrier, inc=1, device_id={"exp": 1 - core}, device_id_type=MESH)
    pl.semaphore_wait(barrier, ctx)

    def remote(src, dst, send, recv, **device):
        return pltpu.make_async_remote_copy(
            src_ref=src, dst_ref=dst, send_sem=send, recv_sem=recv, device_id=device, device_id_type=MESH)

    def row_copy(plane, send, target):
        return remote(rows.at[plane, y], rows.at[plane, y], send, row_recv.at[plane, y], ctx=target)

    def gate_copy(step):
        return remote(gates.at[me], gates.at[me], gate_send.at[step], gate_recv.at[me], ctx=(me + step) % ctx)

    def hop(plane):
        onward = jnp.where(plane < z, z + 1, z - 1)
        return onward, jnp.logical_and(onward >= 0, onward < planes)

    load_rows.wait()

    up = row_copy(z, up_send.at[0], jnp.minimum(z + 1, planes - 1) * 2 + y)
    down = row_copy(z, down_send.at[0], jnp.maximum(z - 1, 0) * 2 + y)

    @pl.when(z + 1 < planes)
    def _():
        up.start()

    @pl.when(z >= 1)
    def _():
        down.start()

    row_copy(z, y_send.at[0], side).start()
    load_gates.wait()
    for step in range(1, ctx):
        gate_copy(step).start()

    def forward(step):
        plane = ordered(z, planes, step)
        row_copy(plane, y_send.at[step], side).wait_recv()
        onward, there = hop(plane)

        @pl.when(there)
        def _():
            row_copy(plane, up_send.at[step], jnp.clip(onward, 0, planes - 1) * 2 + y).start()

        row_copy(plane, y_send.at[step], side).start()

    def core_copy(step):
        return remote(mine.at[step], theirs.at[step], mine_send.at[step], theirs_recv.at[step], exp=1 - core)

    def first(step):
        plane = ordered(z, planes, step)
        remote(rows.at[plane, 1 - y], rows.at[plane, 1 - y], y_send.at[step], row_recv.at[plane, 1 - y],
               ctx=side).wait_recv()

        @pl.loop(0, 2 * fh // TILE)
        def _(tile):
            columns = pl.ds(pl.multiple_of(tile * TILE, TILE), TILE)
            mine[step, :, columns] = jnp.dot(
                rows[plane].reshape(2 * count, width), w_in[:, columns], preferred_element_type=jnp.float32
            ).astype(jnp.bfloat16)

        core_copy(step).start()

    def gate_column(block):
        line = gates[block, pl.ds(z, 1), :]
        shape = (count, count)
        diagonal = lax.broadcasted_iota(jnp.int32, shape, 0) == lax.broadcasted_iota(jnp.int32, shape, 1)
        return jnp.sum(jnp.where(diagonal, jnp.broadcast_to(line, shape), 0.0), axis=1, keepdims=True)

    def second(step):
        plane = ordered(z, planes, step)
        core_copy(step).wait_recv()
        gate = mine[step, :, :fh].astype(jnp.float32) + theirs[step, :, :fh].astype(jnp.float32)
        up_value = mine[step, :, fh:].astype(jnp.float32) + theirs[step, :, fh:].astype(jnp.float32)
        hidden[...] = (jax.nn.silu(gate) * up_value).astype(jnp.bfloat16)
        scale = jnp.concatenate([gate_column(plane * 2), gate_column(plane * 2 + 1)], axis=0)

        @pl.loop(0, width // TILE)
        def _(tile):
            columns = pl.ds(pl.multiple_of(tile * TILE, TILE), TILE)
            out = jnp.dot(hidden[...], w_out[:, columns], preferred_element_type=jnp.float32) * scale
            halves[plane, :, :, columns] = out.astype(jnp.bfloat16).reshape(2, count, TILE)

    def back_copy(step):
        plane = ordered(z, planes, step)
        return remote(halves.at[plane, 1 - y], from_y.at[plane], back_send.at[step], back_recv.at[plane], ctx=side)

    def out_copy(step):
        plane = ordered(z, planes, step)
        return remote(to_z.at[step], from_z.at[z], out_send.at[step], out_recv.at[z], ctx=plane * 2 + y)

    def reduce(step):
        plane = ordered(z, planes, step)
        back_copy(step).wait_recv()
        to_z[step] = (halves[plane, y].astype(jnp.float32) + from_y[plane].astype(jnp.float32)).astype(jnp.bfloat16)
        out_copy(step).start()

    for step in range(planes):
        if step + 1 < planes:
            forward(step + 1)
        if step == 0:
            load_in.wait()
        first(step)
        if step == 0:
            load_out.wait()
            for other in range(1, ctx):
                source = (me + other) % ctx
                remote(gates.at[source], gates.at[source], gate_send.at[other], gate_recv.at[source],
                       ctx=source).wait_recv()
        if step >= 1:
            second(step - 1)
            if step >= 2:
                back_copy(step - 1).start()
    second(planes - 1)
    if planes > 1:
        back_copy(planes - 1).start()
    back_copy(0).start()
    for step in range(1, planes):
        reduce(step)
    back_copy(0).wait_recv()
    for step in range(1, planes):
        plane = ordered(z, planes, step)
        remote(to_z.at[step], from_z.at[plane], out_send.at[step], out_recv.at[plane], ctx=plane * 2 + y).wait_recv()

    @pl.loop(0, width // TILE)
    def _(tile):
        columns = pl.ds(pl.multiple_of(tile * TILE, TILE), TILE)
        total = halves[z, y, :, columns].astype(jnp.float32) + from_y[z, :, columns].astype(jnp.float32)
        for step in range(1, planes):
            total = total + from_z[ordered(z, planes, step), :, columns].astype(jnp.float32)
        mixed_ref[:, columns] = total.astype(jnp.bfloat16)

    @pl.when(z + 1 < planes)
    def _():
        up.wait_send()

    @pl.when(z >= 1)
    def _():
        down.wait_send()

    for step in range(planes):
        plane = ordered(z, planes, step)
        row_copy(plane, y_send.at[step], side).wait_send()
        core_copy(step).wait_send()
        back_copy(step).wait_send()
        if step:
            out_copy(step).wait_send()
            onward, there = hop(plane)

            @pl.when(there)
            def _():
                row_copy(plane, up_send.at[step], jnp.clip(onward, 0, planes - 1) * 2 + y).wait_send()

    for step in range(1, ctx):
        gate_copy(step).wait_send()


def gate_table(route_ids, route_gates, experts):
    lines = -(-experts // 8) * 8
    named = route_ids.T[:, None, :] == jnp.arange(lines, dtype=jnp.int32)[None, :, None]
    return jnp.sum(jnp.where(named, route_gates.T[:, None, :], 0.0), axis=0)


def dense(tokens, route_ids, route_gates, w_in, w_out):
    ctx = lax.axis_size("ctx")
    planes = ctx // 2
    count, width = tokens.shape
    fh = w_out.shape[1]
    gates = gate_table(route_ids, route_gates, planes)
    dma = pltpu.SemaphoreType.DMA
    bf16 = jnp.bfloat16
    hbm = pl.BlockSpec(memory_space=pl.ANY)
    return pl.pallas_call(
        functools.partial(layer_kernel, planes),
        out_shape=jax.ShapeDtypeStruct((count, width), bf16),
        in_specs=[hbm, pl.BlockSpec(memory_space=pltpu.VMEM), hbm, hbm],
        out_specs=pl.BlockSpec(memory_space=pltpu.VMEM),
        scratch_shapes=[
            pltpu.VMEM(w_in.shape[1:], bf16),
            pltpu.VMEM(w_out.shape[1:], bf16),
            pltpu.VMEM((planes, 2, count, width), bf16),
            pltpu.VMEM((ctx,) + gates.shape, jnp.float32),
            pltpu.VMEM((planes, 2 * count, 2 * fh), bf16),
            pltpu.VMEM((planes, 2 * count, 2 * fh), bf16),
            pltpu.VMEM((2 * count, fh), bf16),
            pltpu.VMEM((planes, 2, count, width), bf16),
            pltpu.VMEM((planes, count, width), bf16),
            pltpu.VMEM((planes, count, width), bf16),
            pltpu.VMEM((planes, count, width), bf16),
            dma((4,)), dma((ctx,)), dma((ctx,)), dma((planes, 2)),
            dma((planes,)), dma((1,)), dma((planes,)), dma((planes,)), dma((planes,)),
            dma((planes,)), dma((planes,)), dma((planes,)), dma((planes,)), dma((1,)),
        ],
        compiler_params=pltpu.CompilerParams(
            collective_id=0, has_side_effects=True, vmem_limit_bytes=60 * 1024 * 1024),
        name="experts",
    )(tokens, gates, w_in, w_out)


TILE = 256


def expert_half(rows, w_in, w_out):
    gate_up = jnp.dot(rows, w_in[0], preferred_element_type=jnp.float32)
    summed = lax.psum(gate_up.astype(jnp.bfloat16), "exp").astype(jnp.float32)
    hidden_units = w_out.shape[1]
    hidden = (jax.nn.silu(summed[:, :hidden_units]) * summed[:, hidden_units:]).astype(jnp.bfloat16)
    return jnp.dot(hidden, w_out[0], preferred_element_type=jnp.float32).astype(jnp.bfloat16)


def per_device(tokens, route_ids, route_gates, w_in, w_out):
    ctx_size = lax.axis_size("ctx")
    experts = ctx_size // 2
    tok_rows, half_width = tokens.shape
    top_count = route_ids.shape[1]
    capacity = 2 * ((top_count * tok_rows + experts - 1) // experts)
    if capacity >= tok_rows:
        return dense(tokens, route_ids, route_gates, w_in, w_out)
    slots = experts * capacity
    flat_ids = route_ids.reshape(-1)
    onehot = (flat_ids[:, None] == jnp.arange(experts, dtype=jnp.int32)[None, :]).astype(jnp.int32)
    before = jnp.cumsum(onehot, axis=0) - onehot
    rank = jnp.sum(before * onehot, axis=1)
    slot_of = flat_ids * capacity + rank
    placed = (slot_of[:, None] == jnp.arange(slots, dtype=jnp.int32)[None, :]).astype(jnp.bfloat16)
    placed = placed.reshape(tok_rows, top_count, slots)
    every_map = jnp.sum(placed.astype(jnp.float32), axis=1).astype(jnp.bfloat16)
    gathered = lax.dot_general(
        every_map, tokens, (((0,), (0,)), ((), ())), preferred_element_type=jnp.float32
    ).astype(jnp.bfloat16)
    outgoing = jnp.broadcast_to(
        gathered.reshape(experts, 1, capacity, half_width), (experts, 2, capacity, half_width)
    ).reshape(ctx_size, capacity, half_width)
    received = lax.all_to_all(outgoing, "ctx", split_axis=0, concat_axis=0, tiled=True)
    count = received.shape[1]
    partial_out = expert_half(received.reshape(-1, half_width), w_in, w_out).reshape(
        ctx_size, count, half_width
    )
    returned = lax.all_to_all(partial_out, "ctx", split_axis=0, concat_axis=0, tiled=True)
    results = (
        jnp.sum(returned.astype(jnp.float32).reshape(experts, 2, capacity, half_width), axis=1)
        .astype(jnp.bfloat16)
        .reshape(slots, half_width)
    )
    mixed = jnp.zeros((tok_rows, half_width), jnp.float32)
    for route in range(top_count):
        route_out = jnp.dot(placed[:, route], results, preferred_element_type=jnp.float32)
        mixed = mixed + route_gates[:, route : route + 1] * route_out
    return mixed.astype(jnp.bfloat16)


def solution(mesh):
    placed = (
        P(("groups", "ctx"), "exp"),
        P(("groups", "ctx"), None),
        P(("groups", "ctx"), None),
        P("ctx", "exp", None),
        P("ctx", None, "exp"),
    )
    return jax.shard_map(
        per_device,
        mesh=mesh,
        in_specs=placed,
        out_specs=P(("groups", "ctx"), "exp"),
        check_vma=False,
    )
```

```python
import functools

import jax
import jax.numpy as jnp
from jax import lax
from jax.experimental import pallas as pl
from jax.experimental.pallas import tpu as pltpu
from jax.sharding import PartitionSpec as P

MESH = pl.DeviceIdType.MESH


def ordered(z, planes, step):
    if step == 0:
        return z
    near = jnp.minimum(z, planes - 1 - z)
    paired = jnp.where(step % 2 == 1, z - (step + 1) // 2, z + (step + 1) // 2)
    rest = jnp.where(2 * z < planes - 1, z + step - near, z - step + near)
    return jnp.where(step <= 2 * near, paired, rest)


def layer_kernel(planes, tokens_hbm, gates_ref, w_in_hbm, w_out_hbm, mixed_ref,
                 w_in, w_out, rows, gates, mine, theirs, hidden, halves, from_y, to_z, from_z, total,
                 load_sem, gate_send, gate_recv, row_recv, up_send, down_send, y_send, mine_send, theirs_recv,
                 back_send, back_recv, out_send, out_recv):
    ctx = 2 * planes
    me = lax.axis_index("ctx")
    core = lax.axis_index("exp")
    z, y = me // 2, me % 2
    side = z * 2 + 1 - y
    count, width = tokens_hbm.shape
    fh = w_out.shape[0]
    chunks, span = to_z.shape[1], to_z.shape[3]

    load_rows = pltpu.make_async_copy(tokens_hbm, rows.at[z, y], load_sem.at[0])
    load_in = pltpu.make_async_copy(w_in_hbm.at[0], w_in, load_sem.at[1])
    load_out = pltpu.make_async_copy(w_out_hbm.at[0], w_out, load_sem.at[2])
    load_gates = pltpu.make_async_copy(gates_ref, gates.at[me], load_sem.at[3])
    load_rows.start()
    load_gates.start()
    load_in.start()
    load_out.start()

    barrier = pltpu.get_barrier_semaphore()
    for step in range(1, ctx):
        pl.semaphore_signal(barrier, inc=1, device_id={"ctx": (me + step) % ctx}, device_id_type=MESH)
    pl.semaphore_signal(barrier, inc=1, device_id={"exp": 1 - core}, device_id_type=MESH)
    pl.semaphore_wait(barrier, ctx)

    def remote(src, dst, send, recv, **device):
        return pltpu.make_async_remote_copy(
            src_ref=src, dst_ref=dst, send_sem=send, recv_sem=recv, device_id=device, device_id_type=MESH)

    def row_copy(plane, send, target):
        return remote(rows.at[plane, y], rows.at[plane, y], send, row_recv.at[plane, y], ctx=target)

    def gate_copy(step):
        return remote(gates.at[me], gates.at[me], gate_send.at[step], gate_recv.at[me], ctx=(me + step) % ctx)

    def hop(plane):
        onward = jnp.where(plane < z, z + 1, z - 1)
        return onward, jnp.logical_and(onward >= 0, onward < planes)

    load_rows.wait()

    up = row_copy(z, up_send.at[0], jnp.minimum(z + 1, planes - 1) * 2 + y)
    down = row_copy(z, down_send.at[0], jnp.maximum(z - 1, 0) * 2 + y)

    @pl.when(z + 1 < planes)
    def _():
        up.start()

    @pl.when(z >= 1)
    def _():
        down.start()

    row_copy(z, y_send.at[0], side).start()
    load_gates.wait()
    for step in range(1, ctx):
        gate_copy(step).start()

    def forward(step):
        plane = ordered(z, planes, step)
        row_copy(plane, y_send.at[step], side).wait_recv()
        onward, there = hop(plane)

        @pl.when(there)
        def _():
            row_copy(plane, up_send.at[step], jnp.clip(onward, 0, planes - 1) * 2 + y).start()

        row_copy(plane, y_send.at[step], side).start()

    def core_copy(step):
        return remote(mine.at[step], theirs.at[step], mine_send.at[step], theirs_recv.at[step], exp=1 - core)

    def first(step):
        plane = ordered(z, planes, step)
        remote(rows.at[plane, 1 - y], rows.at[plane, 1 - y], y_send.at[step], row_recv.at[plane, 1 - y],
               ctx=side).wait_recv()

        @pl.loop(0, 2 * fh // TILE)
        def _(tile):
            columns = pl.ds(pl.multiple_of(tile * TILE, TILE), TILE)
            mine[step, :, columns] = jnp.dot(
                rows[plane].reshape(2 * count, width), w_in[:, columns], preferred_element_type=jnp.float32
            ).astype(jnp.bfloat16)
            remote(mine.at[step, :, columns], theirs.at[step, :, columns], mine_send.at[step], theirs_recv.at[step],
                   exp=1 - core).start()


    def gate_column(block):
        line = gates[block, pl.ds(z, 1), :]
        shape = (count, count)
        diagonal = lax.broadcasted_iota(jnp.int32, shape, 0) == lax.broadcasted_iota(jnp.int32, shape, 1)
        return jnp.sum(jnp.where(diagonal, jnp.broadcast_to(line, shape), 0.0), axis=1, keepdims=True)

    def second(step, sends):
        plane = ordered(z, planes, step)
        core_copy(step).wait_recv()
        gate = mine[step, :, :fh].astype(jnp.float32) + theirs[step, :, :fh].astype(jnp.float32)
        up_value = mine[step, :, fh:].astype(jnp.float32) + theirs[step, :, fh:].astype(jnp.float32)
        hidden[...] = (jax.nn.silu(gate) * up_value).astype(jnp.bfloat16)
        scale = jnp.concatenate([gate_column(plane * 2), gate_column(plane * 2 + 1)], axis=0)

        @pl.loop(0, chunks)
        def _(chunk):
            for at in range(0, span, TILE):
                columns = pl.ds(pl.multiple_of(chunk * span + at, TILE), TILE)
                out = jnp.dot(hidden[...], w_out[:, columns], preferred_element_type=jnp.float32) * scale
                halves[plane, :, chunk, :, at:at + TILE] = out.astype(jnp.bfloat16).reshape(2, count, TILE)
            if sends:
                back_copy(step, chunk).start()

    def back_copy(step, chunk):
        plane = ordered(z, planes, step)
        return remote(halves.at[plane, 1 - y, chunk], from_y.at[plane, chunk], back_send.at[step, chunk],
                      back_recv.at[plane, chunk], ctx=side)

    def out_copy(step, chunk):
        plane = ordered(z, planes, step)
        onward = jnp.where(plane > z, z + 1, z - 1)
        slot = jnp.where(jnp.logical_and(onward == plane, plane < z), planes, plane)
        return remote(to_z.at[step, chunk], from_z.at[slot, chunk], out_send.at[step, chunk],
                      out_recv.at[slot, chunk], ctx=onward * 2 + y)

    def wait_chain(slot, chunk):
        remote(to_z.at[0, chunk], from_z.at[slot, chunk], out_send.at[0, chunk], out_recv.at[slot, chunk],
               ctx=side).wait_recv()

    def reduce(step):
        plane = ordered(z, planes, step)
        passes = jnp.where(plane > z, z >= 1, z + 1 < planes)

        @pl.loop(0, chunks)
        def _(chunk):
            back_copy(step, chunk).wait_recv()

            @pl.when(passes)
            def _():
                wait_chain(plane, chunk)
                value = halves[plane, y, chunk].astype(jnp.float32) + from_y[plane, chunk].astype(jnp.float32)
                to_z[step, chunk] = (value + from_z[plane, chunk].astype(jnp.float32)).astype(jnp.bfloat16)

            @pl.when(jnp.logical_not(passes))
            def _():
                value = halves[plane, y, chunk].astype(jnp.float32) + from_y[plane, chunk].astype(jnp.float32)
                to_z[step, chunk] = value.astype(jnp.bfloat16)

            out_copy(step, chunk).start()

    for step in range(planes):
        if step + 1 < planes:
            forward(step + 1)
        if step == 0:
            load_in.wait()
        first(step)
        if step == 0:
            load_out.wait()
            for other in range(1, ctx):
                source = (me + other) % ctx
                remote(gates.at[source], gates.at[source], gate_send.at[other], gate_recv.at[source],
                       ctx=source).wait_recv()
        if 1 <= step < planes - 1:
            second(step - 1, False)
        if step == planes - 2:
            second(step, step >= 1)
    second(planes - 1, planes > 1)

    for step in list(range(planes - 3, 0, -1)) + [0]:
        @pl.loop(0, chunks)
        def _(chunk):
            back_copy(step, chunk).start()

    for step in [planes - 2] * (planes > 2) + [planes - 1] * (planes > 1) + list(range(planes - 3, 0, -1)):
        reduce(step)

    @pl.loop(0, chunks)
    def _(chunk):
        back_copy(0, chunk).wait_recv()
        total[...] = halves[z, y, chunk].astype(jnp.float32) + from_y[z, chunk].astype(jnp.float32)

        @pl.when(z >= 1)
        def _():
            wait_chain(z, chunk)
            total[...] += from_z[z, chunk].astype(jnp.float32)

        @pl.when(z + 1 < planes)
        def _():
            wait_chain(planes, chunk)
            total[...] += from_z[planes, chunk].astype(jnp.float32)

        mixed_ref[:, pl.ds(pl.multiple_of(chunk * span, span), span)] = total[...].astype(jnp.bfloat16)

    @pl.when(z + 1 < planes)
    def _():
        up.wait_send()

    @pl.when(z >= 1)
    def _():
        down.wait_send()

    for step in range(planes):
        plane = ordered(z, planes, step)
        row_copy(plane, y_send.at[step], side).wait_send()
        core_copy(step).wait_send()
        for chunk in range(chunks):
            back_copy(step, chunk).wait_send()
        if step:
            for chunk in range(chunks):
                out_copy(step, chunk).wait_send()
            onward, there = hop(plane)

            @pl.when(there)
            def _():
                row_copy(plane, up_send.at[step], jnp.clip(onward, 0, planes - 1) * 2 + y).wait_send()

    for step in range(1, ctx):
        gate_copy(step).wait_send()


def gate_table(route_ids, route_gates, experts):
    lines = -(-experts // 8) * 8
    named = route_ids.T[:, None, :] == jnp.arange(lines, dtype=jnp.int32)[None, :, None]
    return jnp.sum(jnp.where(named, route_gates.T[:, None, :], 0.0), axis=0)


def dense(tokens, route_ids, route_gates, w_in, w_out):
    ctx = lax.axis_size("ctx")
    planes = ctx // 2
    count, width = tokens.shape
    fh = w_out.shape[1]
    span = SPAN if width % SPAN == 0 else width
    chunks = width // span
    gates = gate_table(route_ids, route_gates, planes)
    dma = pltpu.SemaphoreType.DMA
    bf16 = jnp.bfloat16
    hbm = pl.BlockSpec(memory_space=pl.ANY)
    return pl.pallas_call(
        functools.partial(layer_kernel, planes),
        out_shape=jax.ShapeDtypeStruct((count, width), bf16),
        in_specs=[hbm, pl.BlockSpec(memory_space=pltpu.VMEM), hbm, hbm],
        out_specs=pl.BlockSpec(memory_space=pltpu.VMEM),
        scratch_shapes=[
            pltpu.VMEM(w_in.shape[1:], bf16),
            pltpu.VMEM(w_out.shape[1:], bf16),
            pltpu.VMEM((planes, 2, count, width), bf16),
            pltpu.VMEM((ctx,) + gates.shape, jnp.float32),
            pltpu.VMEM((planes, 2 * count, 2 * fh), bf16),
            pltpu.VMEM((planes, 2 * count, 2 * fh), bf16),
            pltpu.VMEM((2 * count, fh), bf16),
            pltpu.VMEM((planes, 2, chunks, count, span), bf16),
            pltpu.VMEM((planes, chunks, count, span), bf16),
            pltpu.VMEM((planes, chunks, count, span), bf16),
            pltpu.VMEM((planes + 1, chunks, count, span), bf16),
            pltpu.VMEM((count, span), jnp.float32),
            dma((4,)), dma((ctx,)), dma((ctx,)), dma((planes, 2)),
            dma((planes,)), dma((1,)), dma((planes,)), dma((planes,)), dma((planes,)),
            dma((planes, chunks)), dma((planes, chunks)), dma((planes, chunks)), dma((planes + 1, chunks)),
        ],
        compiler_params=pltpu.CompilerParams(
            collective_id=0, has_side_effects=True, vmem_limit_bytes=60 * 1024 * 1024),
        name="experts",
    )(tokens, gates, w_in, w_out)


TILE = 256
SPAN = 512


def expert_half(rows, w_in, w_out):
    gate_up = jnp.dot(rows, w_in[0], preferred_element_type=jnp.float32)
    summed = lax.psum(gate_up.astype(jnp.bfloat16), "exp").astype(jnp.float32)
    hidden_units = w_out.shape[1]
    hidden = (jax.nn.silu(summed[:, :hidden_units]) * summed[:, hidden_units:]).astype(jnp.bfloat16)
    return jnp.dot(hidden, w_out[0], preferred_element_type=jnp.float32).astype(jnp.bfloat16)


def per_device(tokens, route_ids, route_gates, w_in, w_out):
    ctx_size = lax.axis_size("ctx")
    experts = ctx_size // 2
    tok_rows, half_width = tokens.shape
    top_count = route_ids.shape[1]
    capacity = 2 * ((top_count * tok_rows + experts - 1) // experts)
    if capacity >= tok_rows:
        return dense(tokens, route_ids, route_gates, w_in, w_out)
    slots = experts * capacity
    flat_ids = route_ids.reshape(-1)
    onehot = (flat_ids[:, None] == jnp.arange(experts, dtype=jnp.int32)[None, :]).astype(jnp.int32)
    before = jnp.cumsum(onehot, axis=0) - onehot
    rank = jnp.sum(before * onehot, axis=1)
    slot_of = flat_ids * capacity + rank
    placed = (slot_of[:, None] == jnp.arange(slots, dtype=jnp.int32)[None, :]).astype(jnp.bfloat16)
    placed = placed.reshape(tok_rows, top_count, slots)
    every_map = jnp.sum(placed.astype(jnp.float32), axis=1).astype(jnp.bfloat16)
    gathered = lax.dot_general(
        every_map, tokens, (((0,), (0,)), ((), ())), preferred_element_type=jnp.float32
    ).astype(jnp.bfloat16)
    outgoing = jnp.broadcast_to(
        gathered.reshape(experts, 1, capacity, half_width), (experts, 2, capacity, half_width)
    ).reshape(ctx_size, capacity, half_width)
    received = lax.all_to_all(outgoing, "ctx", split_axis=0, concat_axis=0, tiled=True)
    count = received.shape[1]
    partial_out = expert_half(received.reshape(-1, half_width), w_in, w_out).reshape(
        ctx_size, count, half_width
    )
    returned = lax.all_to_all(partial_out, "ctx", split_axis=0, concat_axis=0, tiled=True)
    results = (
        jnp.sum(returned.astype(jnp.float32).reshape(experts, 2, capacity, half_width), axis=1)
        .astype(jnp.bfloat16)
        .reshape(slots, half_width)
    )
    mixed = jnp.zeros((tok_rows, half_width), jnp.float32)
    for route in range(top_count):
        route_out = jnp.dot(placed[:, route], results, preferred_element_type=jnp.float32)
        mixed = mixed + route_gates[:, route : route + 1] * route_out
    return mixed.astype(jnp.bfloat16)


def solution(mesh):
    placed = (
        P(("groups", "ctx"), "exp"),
        P(("groups", "ctx"), None),
        P(("groups", "ctx"), None),
        P("ctx", "exp", None),
        P("ctx", None, "exp"),
    )
    return jax.shard_map(
        per_device,
        mesh=mesh,
        in_specs=placed,
        out_specs=P(("groups", "ctx"), "exp"),
        check_vma=False,
    )
```

```python
import functools

import jax
import jax.numpy as jnp
from jax import lax
from jax.experimental import pallas as pl
from jax.experimental.pallas import tpu as pltpu
from jax.sharding import PartitionSpec as P

MESH = pl.DeviceIdType.MESH


def ordered(z, planes, step):
    if step == 0:
        return z
    near = jnp.minimum(z, planes - 1 - z)
    paired = jnp.where(step % 2 == 1, z - (step + 1) // 2, z + (step + 1) // 2)
    rest = jnp.where(2 * z < planes - 1, z + step - near, z - step + near)
    return jnp.where(step <= 2 * near, paired, rest)


def layer_kernel(planes, tokens_hbm, gates_ref, w_in_hbm, w_out_hbm, mixed_ref,
                 w_in, w_out, rows, gates, mine, theirs, hidden, halves, from_y, to_z, from_z, total, rest,
                 load_sem, gate_send, gate_recv, row_recv, up_send, down_send, relay_send, y_send, mine_send, theirs_recv,
                 back_send, back_recv, out_send, out_recv, rest_send, rest_recv):
    ctx = 2 * planes
    me = lax.axis_index("ctx")
    core = lax.axis_index("exp")
    z, y = me // 2, me % 2
    side = z * 2 + 1 - y
    count, width = tokens_hbm.shape
    fh = w_out.shape[0]
    chunks, span = to_z.shape[1], to_z.shape[3]
    most = count - rest.shape[1]
    pieces = row_recv.shape[2]
    depth = count // pieces

    load_rows = pltpu.make_async_copy(tokens_hbm, rows.at[z, y], load_sem.at[0])
    load_in = pltpu.make_async_copy(w_in_hbm.at[0], w_in, load_sem.at[1])
    load_out = pltpu.make_async_copy(w_out_hbm.at[0], w_out, load_sem.at[2])
    load_gates = pltpu.make_async_copy(gates_ref, gates.at[me], load_sem.at[3])
    load_rows.start()
    load_gates.start()
    load_in.start()
    load_out.start()

    barrier = pltpu.get_barrier_semaphore()
    for step in range(1, ctx):
        pl.semaphore_signal(barrier, inc=1, device_id={"ctx": (me + step) % ctx}, device_id_type=MESH)
    pl.semaphore_signal(barrier, inc=1, device_id={"exp": 1 - core}, device_id_type=MESH)
    pl.semaphore_wait(barrier, ctx)

    def remote(src, dst, send, recv, **device):
        return pltpu.make_async_remote_copy(
            src_ref=src, dst_ref=dst, send_sem=send, recv_sem=recv, device_id=device, device_id_type=MESH)

    def row_copy(plane, column, piece, send, target):
        part = rows.at[plane, column, pl.ds(piece * depth, depth)]
        return remote(part, part, send, row_recv.at[plane, column, piece], ctx=target)

    def wait_rows(plane, column, piece):
        row_copy(plane, column, piece, y_send.at[0, 0], side).wait_recv()

    def gate_copy(step):
        return remote(gates.at[me], gates.at[me], gate_send.at[step], gate_recv.at[me], ctx=(me + step) % ctx)

    def hop(plane):
        onward = jnp.where(plane < z, z + 1, z - 1)
        return onward, jnp.logical_and(onward >= 0, onward < planes)

    load_rows.wait()

    above, below = jnp.minimum(z + 1, planes - 1) * 2 + y, jnp.maximum(z - 1, 0) * 2 + y

    def spread(column, piece, act):
        @pl.when(z + 1 < planes)
        def _():
            act(row_copy(z, column, piece, up_send.at[column, piece], above))

        @pl.when(z >= 1)
        def _():
            act(row_copy(z, column, piece, down_send.at[column, piece], below))

    for piece in range(pieces):
        spread(y, piece, lambda copy: copy.start())
        row_copy(z, y, piece, y_send.at[0, piece], side).start()
    load_gates.wait()
    for step in range(1, ctx):
        gate_copy(step).start()

    def relay(step, column, piece, act):
        plane = ordered(z, planes, step)
        onward, there = hop(plane)

        @pl.when(there)
        def _():
            act(row_copy(plane, column, piece, relay_send.at[step, column, piece],
                         jnp.clip(onward, 0, planes - 1) * 2 + y))

    def forward(step):
        plane = ordered(z, planes, step)
        for piece in range(pieces):
            wait_rows(plane, y, piece)
            relay(step, y, piece, lambda copy: copy.start())
            if piece < pieces - 1:
                row_copy(plane, y, piece, y_send.at[step, piece], side).start()

    def crossed(step):
        plane = ordered(z, planes, step)
        wait_rows(plane, 1 - y, pieces - 1)
        if step == 0:
            spread(1 - y, pieces - 1, lambda copy: copy.start())
        else:
            relay(step, 1 - y, pieces - 1, lambda copy: copy.start())

    def core_copy(step):
        return remote(mine.at[step], theirs.at[step], mine_send.at[step], theirs_recv.at[step], exp=1 - core)

    def first(step):
        plane = ordered(z, planes, step)
        for piece in range(pieces - 1):
            wait_rows(plane, 1 - y, piece)

        @pl.loop(0, 2 * fh // TILE)
        def _(tile):
            columns = pl.ds(pl.multiple_of(tile * TILE, TILE), TILE)
            mine[step, :, columns] = jnp.dot(
                rows[plane].reshape(2 * count, width), w_in[:, columns], preferred_element_type=jnp.float32
            ).astype(jnp.bfloat16)
            remote(mine.at[step, :, columns], theirs.at[step, :, columns], mine_send.at[step], theirs_recv.at[step],
                   exp=1 - core).start()


    def gate_column(block):
        line = gates[block, pl.ds(z, 1), :]
        shape = (count, count)
        diagonal = lax.broadcasted_iota(jnp.int32, shape, 0) == lax.broadcasted_iota(jnp.int32, shape, 1)
        return jnp.sum(jnp.where(diagonal, jnp.broadcast_to(line, shape), 0.0), axis=1, keepdims=True)

    def second(step, sends):
        plane = ordered(z, planes, step)
        core_copy(step).wait_recv()
        gate = mine[step, :, :fh].astype(jnp.float32) + theirs[step, :, :fh].astype(jnp.float32)
        up_value = mine[step, :, fh:].astype(jnp.float32) + theirs[step, :, fh:].astype(jnp.float32)
        hidden[...] = (jax.nn.silu(gate) * up_value).astype(jnp.bfloat16)
        scale = jnp.concatenate([gate_column(plane * 2), gate_column(plane * 2 + 1)], axis=0)

        @pl.loop(0, chunks)
        def _(chunk):
            for at in range(0, span, TILE):
                columns = pl.ds(pl.multiple_of(chunk * span + at, TILE), TILE)
                out = jnp.dot(hidden[...], w_out[:, columns], preferred_element_type=jnp.float32) * scale
                halves[plane, :, chunk, :, at:at + TILE] = out.astype(jnp.bfloat16).reshape(2, count, TILE)
            if sends:
                back_copy(step, chunk).start()

    def back_copy(step, chunk):
        plane = ordered(z, planes, step)
        part = pl.ds(0, most)
        return remote(halves.at[plane, 1 - y, chunk, part], from_y.at[plane, chunk, part], back_send.at[step, chunk],
                      back_recv.at[plane, chunk], ctx=side)

    def out_copy(step, chunk):
        plane = ordered(z, planes, step)
        onward = jnp.where(plane > z, z + 1, z - 1)
        slot = jnp.where(jnp.logical_and(onward == plane, plane < z), planes, plane)
        return remote(to_z.at[step, chunk], from_z.at[slot, chunk], out_send.at[step, chunk],
                      out_recv.at[slot, chunk], ctx=onward * 2 + y)

    def wait_chain(slot, chunk):
        remote(to_z.at[0, chunk], from_z.at[slot, chunk], out_send.at[0, chunk], out_recv.at[slot, chunk],
               ctx=side).wait_recv()

    def reduce(step):
        plane = ordered(z, planes, step)
        passes = jnp.where(plane > z, z >= 1, z + 1 < planes)

        @pl.loop(0, chunks)
        def _(chunk):
            back_copy(step, chunk).wait_recv()

            @pl.when(passes)
            def _():
                wait_chain(plane, chunk)

            def put(first, last, value):
                @pl.when(passes)
                def _():
                    chained = value + from_z[plane, chunk, first:last].astype(jnp.float32)
                    to_z[step, chunk, first:last] = chained.astype(jnp.bfloat16)

                @pl.when(jnp.logical_not(passes))
                def _():
                    to_z[step, chunk, first:last] = value.astype(jnp.bfloat16)

            own = halves[plane, y, chunk].astype(jnp.float32)
            put(0, most, own[:most] + from_y[plane, chunk, :most].astype(jnp.float32))
            put(most, count, own[most:])
            put(count, 2 * count - most, halves[plane, 1 - y, chunk, most:].astype(jnp.float32))
            out_copy(step, chunk).start()

    def rest_copy(chunk):
        return remote(rest.at[chunk], from_y.at[z, chunk, pl.ds(most, count - most)], rest_send.at[chunk],
                      rest_recv.at[chunk], ctx=side)

    for step in range(planes):
        crossed(step)
        if step + 1 < planes:
            forward(step + 1)
        if step == 0:
            load_in.wait()
        first(step)
        if step == 0:
            load_out.wait()
            for other in range(1, ctx):
                source = (me + other) % ctx
                remote(gates.at[source], gates.at[source], gate_send.at[other], gate_recv.at[source],
                       ctx=source).wait_recv()
        if 1 <= step < planes - 1:
            second(step - 1, False)
        if step == planes - 2:
            second(step, step >= 1)
    second(planes - 1, planes > 1)

    for step in list(range(planes - 3, 0, -1)) + [0]:
        @pl.loop(0, chunks)
        def _(chunk):
            back_copy(step, chunk).start()

    for step in [planes - 2] * (planes > 2) + [planes - 1] * (planes > 1) + list(range(planes - 3, 0, -1)):
        reduce(step)

    def chains(first, last, chunk, act):
        @pl.when(z >= 1)
        def _():
            act(z)
            total[first:last] += from_z[z, chunk, first:last].astype(jnp.float32)

        @pl.when(z + 1 < planes)
        def _():
            act(planes)
            total[first:last] += from_z[planes, chunk, first:last].astype(jnp.float32)

    @pl.loop(0, chunks)
    def _(chunk):
        total[count:] = halves[z, 1 - y, chunk, most:].astype(jnp.float32)
        chains(count, 2 * count - most, chunk, lambda slot: wait_chain(slot, chunk))
        rest[chunk] = total[count:].astype(jnp.bfloat16)
        rest_copy(chunk).start()

    @pl.loop(0, chunks)
    def _(chunk):
        back_copy(0, chunk).wait_recv()
        rest_copy(chunk).wait_recv()
        total[:count] = halves[z, y, chunk].astype(jnp.float32) + from_y[z, chunk].astype(jnp.float32)
        chains(0, count, chunk, lambda slot: None)
        mixed_ref[:, pl.ds(pl.multiple_of(chunk * span, span), span)] = total[:count].astype(jnp.bfloat16)

    finish = lambda copy: copy.wait_send()
    for piece in range(pieces):
        spread(y, piece, finish)
    spread(1 - y, pieces - 1, finish)
    for chunk in range(chunks):
        rest_copy(chunk).wait_send()
    for step in range(planes):
        plane = ordered(z, planes, step)
        for piece in range(pieces - (step > 0)):
            row_copy(plane, y, piece, y_send.at[step, piece], side).wait_send()
        core_copy(step).wait_send()
        for chunk in range(chunks):
            back_copy(step, chunk).wait_send()
        if step:
            for chunk in range(chunks):
                out_copy(step, chunk).wait_send()
            for piece in range(pieces):
                relay(step, y, piece, finish)
            relay(step, 1 - y, pieces - 1, finish)

    for step in range(1, ctx):
        gate_copy(step).wait_send()


def gate_table(route_ids, route_gates, experts):
    lines = -(-experts // 8) * 8
    named = route_ids.T[:, None, :] == jnp.arange(lines, dtype=jnp.int32)[None, :, None]
    return jnp.sum(jnp.where(named, route_gates.T[:, None, :], 0.0), axis=0)


def dense(tokens, route_ids, route_gates, w_in, w_out):
    ctx = lax.axis_size("ctx")
    planes = ctx // 2
    count, width = tokens.shape
    fh = w_out.shape[1]
    span = SPAN if width % SPAN == 0 else width
    chunks = width // span
    pieces = PIECES if count % (16 * PIECES) == 0 else 1
    late = max(16, count * LATE // 128 // 16 * 16)
    gates = gate_table(route_ids, route_gates, planes)
    dma = pltpu.SemaphoreType.DMA
    bf16 = jnp.bfloat16
    hbm = pl.BlockSpec(memory_space=pl.ANY)
    return pl.pallas_call(
        functools.partial(layer_kernel, planes),
        out_shape=jax.ShapeDtypeStruct((count, width), bf16),
        in_specs=[hbm, pl.BlockSpec(memory_space=pltpu.VMEM), hbm, hbm],
        out_specs=pl.BlockSpec(memory_space=pltpu.VMEM),
        scratch_shapes=[
            pltpu.VMEM(w_in.shape[1:], bf16),
            pltpu.VMEM(w_out.shape[1:], bf16),
            pltpu.VMEM((planes, 2, count, width), bf16),
            pltpu.VMEM((ctx,) + gates.shape, jnp.float32),
            pltpu.VMEM((planes, 2 * count, 2 * fh), bf16),
            pltpu.VMEM((planes, 2 * count, 2 * fh), bf16),
            pltpu.VMEM((2 * count, fh), bf16),
            pltpu.VMEM((planes, 2, chunks, count, span), bf16),
            pltpu.VMEM((planes, chunks, count, span), bf16),
            pltpu.VMEM((planes, chunks, count + late, span), bf16),
            pltpu.VMEM((planes + 1, chunks, count + late, span), bf16),
            pltpu.VMEM((count + late, span), jnp.float32),
            pltpu.VMEM((chunks, late, span), bf16),
            dma((4,)), dma((ctx,)), dma((ctx,)), dma((planes, 2, pieces)),
            dma((2, pieces)), dma((2, pieces)), dma((planes, 2, pieces)), dma((planes, pieces)), dma((planes,)), dma((planes,)),
            dma((planes, chunks)), dma((planes, chunks)), dma((planes, chunks)), dma((planes + 1, chunks)),
            dma((chunks,)), dma((chunks,)),
        ],
        compiler_params=pltpu.CompilerParams(
            collective_id=0, has_side_effects=True, vmem_limit_bytes=60 * 1024 * 1024),
        name="experts",
    )(tokens, gates, w_in, w_out)


TILE = 256
SPAN = 512
PIECES = 4
LATE = 32


def expert_half(rows, w_in, w_out):
    gate_up = jnp.dot(rows, w_in[0], preferred_element_type=jnp.float32)
    summed = lax.psum(gate_up.astype(jnp.bfloat16), "exp").astype(jnp.float32)
    hidden_units = w_out.shape[1]
    hidden = (jax.nn.silu(summed[:, :hidden_units]) * summed[:, hidden_units:]).astype(jnp.bfloat16)
    return jnp.dot(hidden, w_out[0], preferred_element_type=jnp.float32).astype(jnp.bfloat16)


def per_device(tokens, route_ids, route_gates, w_in, w_out):
    ctx_size = lax.axis_size("ctx")
    experts = ctx_size // 2
    tok_rows, half_width = tokens.shape
    top_count = route_ids.shape[1]
    capacity = 2 * ((top_count * tok_rows + experts - 1) // experts)
    if capacity >= tok_rows:
        return dense(tokens, route_ids, route_gates, w_in, w_out)
    slots = experts * capacity
    flat_ids = route_ids.reshape(-1)
    onehot = (flat_ids[:, None] == jnp.arange(experts, dtype=jnp.int32)[None, :]).astype(jnp.int32)
    before = jnp.cumsum(onehot, axis=0) - onehot
    rank = jnp.sum(before * onehot, axis=1)
    slot_of = flat_ids * capacity + rank
    placed = (slot_of[:, None] == jnp.arange(slots, dtype=jnp.int32)[None, :]).astype(jnp.bfloat16)
    placed = placed.reshape(tok_rows, top_count, slots)
    every_map = jnp.sum(placed.astype(jnp.float32), axis=1).astype(jnp.bfloat16)
    gathered = lax.dot_general(
        every_map, tokens, (((0,), (0,)), ((), ())), preferred_element_type=jnp.float32
    ).astype(jnp.bfloat16)
    outgoing = jnp.broadcast_to(
        gathered.reshape(experts, 1, capacity, half_width), (experts, 2, capacity, half_width)
    ).reshape(ctx_size, capacity, half_width)
    received = lax.all_to_all(outgoing, "ctx", split_axis=0, concat_axis=0, tiled=True)
    count = received.shape[1]
    partial_out = expert_half(received.reshape(-1, half_width), w_in, w_out).reshape(
        ctx_size, count, half_width
    )
    returned = lax.all_to_all(partial_out, "ctx", split_axis=0, concat_axis=0, tiled=True)
    results = (
        jnp.sum(returned.astype(jnp.float32).reshape(experts, 2, capacity, half_width), axis=1)
        .astype(jnp.bfloat16)
        .reshape(slots, half_width)
    )
    mixed = jnp.zeros((tok_rows, half_width), jnp.float32)
    for route in range(top_count):
        route_out = jnp.dot(placed[:, route], results, preferred_element_type=jnp.float32)
        mixed = mixed + route_gates[:, route : route + 1] * route_out
    return mixed.astype(jnp.bfloat16)


def solution(mesh):
    placed = (
        P(("groups", "ctx"), "exp"),
        P(("groups", "ctx"), None),
        P(("groups", "ctx"), None),
        P("ctx", "exp", None),
        P("ctx", None, "exp"),
    )
    return jax.shard_map(
        per_device,
        mesh=mesh,
        in_specs=placed,
        out_specs=P(("groups", "ctx"), "exp"),
        check_vma=False,
    )
```

```python
import functools

import jax
import jax.numpy as jnp
from jax import lax
from jax.experimental import pallas as pl
from jax.experimental.pallas import tpu as pltpu
from jax.sharding import PartitionSpec as P

MESH = pl.DeviceIdType.MESH


def ordered(z, planes, step):
    if step == 0:
        return z
    near = jnp.minimum(z, planes - 1 - z)
    paired = jnp.where(step % 2 == 1, z - (step + 1) // 2, z + (step + 1) // 2)
    rest = jnp.where(2 * z < planes - 1, z + step - near, z - step + near)
    return jnp.where(step <= 2 * near, paired, rest)


def layer_kernel(planes, tokens_hbm, gates_ref, w_in_hbm, w_out_hbm, mixed_ref,
                 w_in, w_out, rows, gates, mine, theirs, hidden, halves, from_y, to_z, from_z, total,
                 load_sem, gate_send, gate_recv, row_recv, up_send, down_send, y_send, mine_send, theirs_recv,
                 back_send, back_recv, out_send, out_recv):
    ctx = 2 * planes
    me = lax.axis_index("ctx")
    core = lax.axis_index("exp")
    z, y = me // 2, me % 2
    side = z * 2 + 1 - y
    count, width = tokens_hbm.shape
    fh = w_out.shape[0]
    chunks, span = to_z.shape[1], to_z.shape[3]

    load_rows = pltpu.make_async_copy(tokens_hbm, rows.at[z, y], load_sem.at[0])
    load_in = pltpu.make_async_copy(w_in_hbm.at[0], w_in, load_sem.at[1])
    load_out = pltpu.make_async_copy(w_out_hbm.at[0], w_out, load_sem.at[2])
    load_gates = pltpu.make_async_copy(gates_ref, gates.at[me], load_sem.at[3])
    load_rows.start()
    load_gates.start()
    load_in.start()
    load_out.start()

    barrier = pltpu.get_barrier_semaphore()
    for step in range(1, ctx):
        pl.semaphore_signal(barrier, inc=1, device_id={"ctx": (me + step) % ctx}, device_id_type=MESH)
    pl.semaphore_signal(barrier, inc=1, device_id={"exp": 1 - core}, device_id_type=MESH)
    pl.semaphore_wait(barrier, ctx)

    def remote(src, dst, send, recv, **device):
        return pltpu.make_async_remote_copy(
            src_ref=src, dst_ref=dst, send_sem=send, recv_sem=recv, device_id=device, device_id_type=MESH)

    def row_copy(plane, send, target):
        return remote(rows.at[plane, y], rows.at[plane, y], send, row_recv.at[plane, y], ctx=target)

    def gate_copy(step):
        return remote(gates.at[me], gates.at[me], gate_send.at[step], gate_recv.at[me], ctx=(me + step) % ctx)

    def hop(plane):
        onward = jnp.where(plane < z, z + 1, z - 1)
        return onward, jnp.logical_and(onward >= 0, onward < planes)

    load_rows.wait()

    up = row_copy(z, up_send.at[0], jnp.minimum(z + 1, planes - 1) * 2 + y)
    down = row_copy(z, down_send.at[0], jnp.maximum(z - 1, 0) * 2 + y)

    @pl.when(z + 1 < planes)
    def _():
        up.start()

    @pl.when(z >= 1)
    def _():
        down.start()

    row_copy(z, y_send.at[0], side).start()
    load_gates.wait()
    for step in range(1, ctx):
        gate_copy(step).start()

    def forward(step):
        plane = ordered(z, planes, step)
        row_copy(plane, y_send.at[step], side).wait_recv()
        onward, there = hop(plane)

        @pl.when(there)
        def _():
            row_copy(plane, up_send.at[step], jnp.clip(onward, 0, planes - 1) * 2 + y).start()

        row_copy(plane, y_send.at[step], side).start()

    def core_copy(step):
        return remote(mine.at[step], theirs.at[step], mine_send.at[step], theirs_recv.at[step], exp=1 - core)

    def first(step):
        plane = ordered(z, planes, step)
        remote(rows.at[plane, 1 - y], rows.at[plane, 1 - y], y_send.at[step], row_recv.at[plane, 1 - y],
               ctx=side).wait_recv()

        @pl.loop(0, 2 * fh // TILE)
        def _(tile):
            columns = pl.ds(pl.multiple_of(tile * TILE, TILE), TILE)
            mine[step, :, columns] = jnp.dot(
                rows[plane].reshape(2 * count, width), w_in[:, columns], preferred_element_type=jnp.float32
            ).astype(jnp.bfloat16)
            remote(mine.at[step, :, columns], theirs.at[step, :, columns], mine_send.at[step], theirs_recv.at[step],
                   exp=1 - core).start()


    def gate_column(block):
        line = gates[block, pl.ds(z, 1), :]
        shape = (count, count)
        diagonal = lax.broadcasted_iota(jnp.int32, shape, 0) == lax.broadcasted_iota(jnp.int32, shape, 1)
        return jnp.sum(jnp.where(diagonal, jnp.broadcast_to(line, shape), 0.0), axis=1, keepdims=True)

    def second(step, sends):
        plane = ordered(z, planes, step)
        core_copy(step).wait_recv()
        gate = mine[step, :, :fh].astype(jnp.float32) + theirs[step, :, :fh].astype(jnp.float32)
        up_value = mine[step, :, fh:].astype(jnp.float32) + theirs[step, :, fh:].astype(jnp.float32)
        hidden[...] = (jax.nn.silu(gate) * up_value).astype(jnp.bfloat16)
        scale = jnp.concatenate([gate_column(plane * 2), gate_column(plane * 2 + 1)], axis=0)

        @pl.loop(0, chunks)
        def _(chunk):
            for at in range(0, span, TILE):
                columns = pl.ds(pl.multiple_of(chunk * span + at, TILE), TILE)
                out = jnp.dot(hidden[...], w_out[:, columns], preferred_element_type=jnp.float32) * scale
                halves[plane, :, chunk, :, at:at + TILE] = out.astype(jnp.bfloat16).reshape(2, count, TILE)
            if sends:
                back_copy(step, chunk).start()

    def back_copy(step, chunk):
        plane = ordered(z, planes, step)
        return remote(halves.at[plane, 1 - y, chunk], from_y.at[plane, chunk], back_send.at[step, chunk],
                      back_recv.at[plane, chunk], ctx=side)

    def out_copy(step, chunk):
        plane = ordered(z, planes, step)
        onward = jnp.where(plane > z, z + 1, z - 1)
        slot = jnp.where(jnp.logical_and(onward == plane, plane < z), planes, plane)
        return remote(to_z.at[step, chunk], from_z.at[slot, chunk], out_send.at[step, chunk],
                      out_recv.at[slot, chunk], ctx=onward * 2 + y)

    def wait_chain(slot, chunk):
        remote(to_z.at[0, chunk], from_z.at[slot, chunk], out_send.at[0, chunk], out_recv.at[slot, chunk],
               ctx=side).wait_recv()

    def reduce(step):
        plane = ordered(z, planes, step)
        passes = jnp.where(plane > z, z >= 1, z + 1 < planes)

        @pl.loop(0, chunks)
        def _(chunk):
            back_copy(step, chunk).wait_recv()

            @pl.when(passes)
            def _():
                wait_chain(plane, chunk)
                value = halves[plane, y, chunk].astype(jnp.float32) + from_y[plane, chunk].astype(jnp.float32)
                to_z[step, chunk] = (value + from_z[plane, chunk].astype(jnp.float32)).astype(jnp.bfloat16)

            @pl.when(jnp.logical_not(passes))
            def _():
                value = halves[plane, y, chunk].astype(jnp.float32) + from_y[plane, chunk].astype(jnp.float32)
                to_z[step, chunk] = value.astype(jnp.bfloat16)

            out_copy(step, chunk).start()

    for step in range(planes):
        if step + 1 < planes:
            forward(step + 1)
        if step == 0:
            load_in.wait()
        first(step)
        if step == 0:
            load_out.wait()
            for other in range(1, ctx):
                source = (me + other) % ctx
                remote(gates.at[source], gates.at[source], gate_send.at[other], gate_recv.at[source],
                       ctx=source).wait_recv()
        if 1 <= step < planes - 1:
            second(step - 1, False)
        if step == planes - 2:
            second(step, step >= 1)
    second(planes - 1, planes > 1)

    for step in list(range(planes - 3, 0, -1)) + [0]:
        @pl.loop(0, chunks)
        def _(chunk):
            back_copy(step, chunk).start()

    for step in range(planes - 1, 0, -1):
        reduce(step)

    @pl.loop(0, chunks)
    def _(chunk):
        back_copy(0, chunk).wait_recv()
        total[...] = halves[z, y, chunk].astype(jnp.float32) + from_y[z, chunk].astype(jnp.float32)

        @pl.when(z >= 1)
        def _():
            wait_chain(z, chunk)
            total[...] += from_z[z, chunk].astype(jnp.float32)

        @pl.when(z + 1 < planes)
        def _():
            wait_chain(planes, chunk)
            total[...] += from_z[planes, chunk].astype(jnp.float32)

        mixed_ref[:, pl.ds(pl.multiple_of(chunk * span, span), span)] = total[...].astype(jnp.bfloat16)

    @pl.when(z + 1 < planes)
    def _():
        up.wait_send()

    @pl.when(z >= 1)
    def _():
        down.wait_send()

    for step in range(planes):
        plane = ordered(z, planes, step)
        row_copy(plane, y_send.at[step], side).wait_send()
        core_copy(step).wait_send()
        for chunk in range(chunks):
            back_copy(step, chunk).wait_send()
        if step:
            for chunk in range(chunks):
                out_copy(step, chunk).wait_send()
            onward, there = hop(plane)

            @pl.when(there)
            def _():
                row_copy(plane, up_send.at[step], jnp.clip(onward, 0, planes - 1) * 2 + y).wait_send()

    for step in range(1, ctx):
        gate_copy(step).wait_send()


def gate_table(route_ids, route_gates, experts):
    lines = -(-experts // 8) * 8
    named = route_ids.T[:, None, :] == jnp.arange(lines, dtype=jnp.int32)[None, :, None]
    return jnp.sum(jnp.where(named, route_gates.T[:, None, :], 0.0), axis=0)


def dense(tokens, route_ids, route_gates, w_in, w_out):
    ctx = lax.axis_size("ctx")
    planes = ctx // 2
    count, width = tokens.shape
    fh = w_out.shape[1]
    span = SPAN if width % SPAN == 0 else width
    chunks = width // span
    gates = gate_table(route_ids, route_gates, planes)
    dma = pltpu.SemaphoreType.DMA
    bf16 = jnp.bfloat16
    hbm = pl.BlockSpec(memory_space=pl.ANY)
    return pl.pallas_call(
        functools.partial(layer_kernel, planes),
        out_shape=jax.ShapeDtypeStruct((count, width), bf16),
        in_specs=[hbm, pl.BlockSpec(memory_space=pltpu.VMEM), hbm, hbm],
        out_specs=pl.BlockSpec(memory_space=pltpu.VMEM),
        scratch_shapes=[
            pltpu.VMEM(w_in.shape[1:], bf16),
            pltpu.VMEM(w_out.shape[1:], bf16),
            pltpu.VMEM((planes, 2, count, width), bf16),
            pltpu.VMEM((ctx,) + gates.shape, jnp.float32),
            pltpu.VMEM((planes, 2 * count, 2 * fh), bf16),
            pltpu.VMEM((planes, 2 * count, 2 * fh), bf16),
            pltpu.VMEM((2 * count, fh), bf16),
            pltpu.VMEM((planes, 2, chunks, count, span), bf16),
            pltpu.VMEM((planes, chunks, count, span), bf16),
            pltpu.VMEM((planes, chunks, count, span), bf16),
            pltpu.VMEM((planes + 1, chunks, count, span), bf16),
            pltpu.VMEM((count, span), jnp.float32),
            dma((4,)), dma((ctx,)), dma((ctx,)), dma((planes, 2)),
            dma((planes,)), dma((1,)), dma((planes,)), dma((planes,)), dma((planes,)),
            dma((planes, chunks)), dma((planes, chunks)), dma((planes, chunks)), dma((planes + 1, chunks)),
        ],
        compiler_params=pltpu.CompilerParams(
            collective_id=0, has_side_effects=True, vmem_limit_bytes=60 * 1024 * 1024),
        name="experts",
    )(tokens, gates, w_in, w_out)


TILE = 256
SPAN = 512


def expert_half(rows, w_in, w_out):
    gate_up = jnp.dot(rows, w_in[0], preferred_element_type=jnp.float32)
    summed = lax.psum(gate_up.astype(jnp.bfloat16), "exp").astype(jnp.float32)
    hidden_units = w_out.shape[1]
    hidden = (jax.nn.silu(summed[:, :hidden_units]) * summed[:, hidden_units:]).astype(jnp.bfloat16)
    return jnp.dot(hidden, w_out[0], preferred_element_type=jnp.float32).astype(jnp.bfloat16)


def per_device(tokens, route_ids, route_gates, w_in, w_out):
    ctx_size = lax.axis_size("ctx")
    experts = ctx_size // 2
    tok_rows, half_width = tokens.shape
    top_count = route_ids.shape[1]
    capacity = 2 * ((top_count * tok_rows + experts - 1) // experts)
    if capacity >= tok_rows:
        return dense(tokens, route_ids, route_gates, w_in, w_out)
    slots = experts * capacity
    flat_ids = route_ids.reshape(-1)
    onehot = (flat_ids[:, None] == jnp.arange(experts, dtype=jnp.int32)[None, :]).astype(jnp.int32)
    before = jnp.cumsum(onehot, axis=0) - onehot
    rank = jnp.sum(before * onehot, axis=1)
    slot_of = flat_ids * capacity + rank
    placed = (slot_of[:, None] == jnp.arange(slots, dtype=jnp.int32)[None, :]).astype(jnp.bfloat16)
    placed = placed.reshape(tok_rows, top_count, slots)
    every_map = jnp.sum(placed.astype(jnp.float32), axis=1).astype(jnp.bfloat16)
    gathered = lax.dot_general(
        every_map, tokens, (((0,), (0,)), ((), ())), preferred_element_type=jnp.float32
    ).astype(jnp.bfloat16)
    outgoing = jnp.broadcast_to(
        gathered.reshape(experts, 1, capacity, half_width), (experts, 2, capacity, half_width)
    ).reshape(ctx_size, capacity, half_width)
    received = lax.all_to_all(outgoing, "ctx", split_axis=0, concat_axis=0, tiled=True)
    count = received.shape[1]
    partial_out = expert_half(received.reshape(-1, half_width), w_in, w_out).reshape(
        ctx_size, count, half_width
    )
    returned = lax.all_to_all(partial_out, "ctx", split_axis=0, concat_axis=0, tiled=True)
    results = (
        jnp.sum(returned.astype(jnp.float32).reshape(experts, 2, capacity, half_width), axis=1)
        .astype(jnp.bfloat16)
        .reshape(slots, half_width)
    )
    mixed = jnp.zeros((tok_rows, half_width), jnp.float32)
    for route in range(top_count):
        route_out = jnp.dot(placed[:, route], results, preferred_element_type=jnp.float32)
        mixed = mixed + route_gates[:, route : route + 1] * route_out
    return mixed.astype(jnp.bfloat16)


def solution(mesh):
    placed = (
        P(("groups", "ctx"), "exp"),
        P(("groups", "ctx"), None),
        P(("groups", "ctx"), None),
        P("ctx", "exp", None),
        P("ctx", None, "exp"),
    )
    return jax.shard_map(
        per_device,
        mesh=mesh,
        in_specs=placed,
        out_specs=P(("groups", "ctx"), "exp"),
        check_vma=False,
    )
```
